32 devices in a mesh: row: 4 (over y, x), col: 8 (over z, core).
Axes of the slice: x: 2, y: 2, z: 4, core: 2. Of those that a mesh axis runs over, the one named last changes fastest.
Arguments:
- inverses: bfloat16 [4, 32, 1024, 1024], P('row', 'col'), as said below
- coupling: bfloat16 [4, 32, 1024, 256], P('row', 'col'), may hold values from -0.1875 to 0.1875
- orders: int32 [4, 32], P('row', 'col'), may hold values from 512 to 1024, as said below
- owners: int32 [4, 32, 1], P(None, 'col'), may hold values from 0 to 3, as said below
- offsets: int32 [4, 32, 2], P(None, 'col'), may hold values from 0 to 2
- dense_slab: float32 [2048, 4096], P('row', 'col'), may hold values from -6 to 6
- pivots: float32 [1024], replicated, may hold values from 16 to 128
Outputs:
- result: float32 [2048, 4096], P('row', 'col')
The draws below stay inside these ranges and needn't reach their ends.
Inputs may be any that keep to these rules, and one draw needn't show every extreme that they name: `orders`: order of each subdomain; some subdomain has exactly 1024. `owners`: within the 4 subdomains of one device (entries r, s with the same r and the same s // 4) no row block is named twice. `inverses`: each inverse is symmetric.
All inputs are finite; a program needn't handle non-finite values.
Results may differ from the reference program's by a relative error of at most 0.0035.
Values may be sent and summed in bfloat16 or wider, within the bound.
A program may use at most 64 MiB of HBM per device.

```python
import math
import jax
import jax.numpy as jnp
from jax import lax

ORD = 1024
KC = 256
TILE = 512
PW = 1024
SUBS = 4
NSUB_ROW = 32
OFF_UNIT = 128
ROWS = 2048
COLS = 4096
N_ROW = 4


def draw_inverses(key, part):
    shape = (N_ROW, NSUB_ROW, ORD, ORD)
    noise = jax.random.normal(key, shape, jnp.float32)
    symmetric = (noise + jnp.swapaxes(noise, 2, 3)) * (0.6 / ORD ** 0.5)
    identity = jnp.eye(ORD, dtype=jnp.float32)
    return (symmetric + identity).astype(jnp.bfloat16)


def draw_orders(key, part):
    values = jax.random.randint(key, (N_ROW, NSUB_ROW), ORD // 2, ORD + 1, jnp.int32)
    return values.at[0, 0].set(ORD)


def draw_owners(key, part):
    device_count = N_ROW * (NSUB_ROW // SUBS)
    device_keys = jax.random.split(jax.random.fold_in(key, 7), device_count)

    def pick(one_key):
        return jax.random.permutation(one_key, N_ROW)[:SUBS].astype(jnp.int32)
    chosen = jax.vmap(pick)(device_keys)
    return chosen.reshape(N_ROW, NSUB_ROW, 1)


def set_ends(array, rng, smallest, high):
    place = [jax.random.randint(jax.random.fold_in(rng, axis), (), 0, length) for axis, length in enumerate(array.shape)]
    widest = array.shape.index(max(array.shape))
    neighbour = place[:widest] + [(place[widest] + 1) % array.shape[widest]] + place[widest + 1:]
    return array.at[tuple(place)].set(smallest).at[tuple(neighbour)].set(high)


def levels(rng, dims, cuts, least, top_value):
    def one(dim, blocks):
        steps = jax.random.uniform(jax.random.fold_in(jax.random.fold_in(rng, 6), dim), (blocks,), jnp.float32, least / len(cuts), top_value / len(cuts))
        return jnp.repeat(jnp.exp(steps), dims[dim] // blocks).reshape((-1,) + (1,) * (len(dims) - dim - 1))

    loudness = one(*cuts[0])
    for cut in cuts[1:]:
        loudness = loudness * one(*cut)
    return loudness


def bell_draw(stream_key, shape, width, limit, shards=(), kind=jnp.bfloat16):
    entries = width * jax.random.normal(stream_key, shape, jnp.float32)
    if shards:
        entries = entries * levels(stream_key, shape, shards, -0.22, 0.18)
    return jnp.clip(entries, -limit, limit).astype(kind)


def setup_inputs(seed: int = 0) -> dict:
    seeds = jax.random.split(jax.random.key(seed), 8)
    return {
        "inverses": draw_inverses(jax.random.fold_in(seeds[7], 71), 0),
        "coupling": bell_draw(seeds[1], (N_ROW, NSUB_ROW, ORD, KC), ORD ** -0.5, 0.1875, ((0, 4), (1, 8))),
        "orders": draw_orders(jax.random.fold_in(seeds[7], 71), 0),
        "owners": draw_owners(jax.random.fold_in(seeds[7], 71), 0),
        "offsets": set_ends(jax.random.randint(seeds[4], (N_ROW, NSUB_ROW, 2), 0, 3), jax.random.fold_in(seeds[4], 1), 0, 2).astype(jnp.int32),
        "dense_slab": bell_draw(seeds[5], (ROWS, COLS), 1.0, 6.0, ((0, 4), (1, 8)), jnp.float32),
        "pivots": jnp.clip(jnp.exp(jax.random.uniform(seeds[6], (PW,), jnp.float32, math.log(16.0), math.log(128.0))), 16.0, 128.0),
    }


def make_tile(inverse, coupling_cols, order_size):
    live_rows = jnp.arange(inverse.shape[0], dtype=jnp.int32)[:, None] < order_size
    masked = jnp.where(live_rows, coupling_cols, jnp.zeros_like(coupling_cols))
    solved = jnp.dot(inverse.astype(jnp.float32), masked.astype(jnp.float32)).astype(jnp.bfloat16)
    return jnp.dot(masked.astype(jnp.float32).T, solved.astype(jnp.float32)).astype(jnp.bfloat16)


def reference(inverses, coupling, orders, owners, offsets, dense_slab, pivots):
    def add_one(counter, schur_sum):
        row_index = counter // NSUB_ROW
        sub_index = counter % NSUB_ROW
        tile_value = make_tile(inverses[row_index, sub_index], coupling[row_index, sub_index], orders[row_index, sub_index])
        row_start = (owners[row_index, sub_index, 0] * TILE + offsets[row_index, sub_index, 0] * OFF_UNIT).astype(jnp.int32)
        col_start = ((sub_index // SUBS) * TILE + offsets[row_index, sub_index, 1] * OFF_UNIT).astype(jnp.int32)
        current = lax.dynamic_slice(schur_sum, (row_start, col_start), (KC, KC))
        return lax.dynamic_update_slice(schur_sum, current + tile_value.astype(schur_sum.dtype), (row_start, col_start))

    schur_sum = lax.fori_loop(0, N_ROW * NSUB_ROW, add_one, jnp.zeros(dense_slab.shape, jnp.float32))
    updated = dense_slab - schur_sum
    panel = updated[:PW].astype(jnp.bfloat16)
    left_factor = (panel[:, :N_ROW * TILE].astype(jnp.float32) / pivots[:, None]).astype(jnp.bfloat16)
    return updated - jnp.dot(left_factor.astype(jnp.float32).T, panel.astype(jnp.float32))
```

```python
import functools
import jax
import jax.numpy as jnp
from jax import lax
from jax.experimental import pallas as pl
from jax.experimental.pallas import tpu as pltpu
from jax.sharding import PartitionSpec as P

MESH = pl.DeviceIdType.MESH
BF16 = jnp.bfloat16
F32 = jnp.float32
CHUNKS = 8
GROUPS = 2
AB = 256


def contract0(a, b):
    return lax.dot_general(a, b, (((0,), (0,)), ((), ())), preferred_element_type=F32)


def kernel(
    dims,
    inv_hbm, cpl_hbm, orders, owners, offsets, slab_hbm, pivots,
    out,
    a_buf, m_buf, slab, mm, sol, tiles, send, recv, panel, left, piv,
    a_sem, m_sem, s_sem, t_send, t_recv, ax_send, ay_send, g_recv,
    up_send, dn_send, core_send, l_recv,
):
    rows, cols, subs, order, width, tile = dims
    unit = (tile - width) // 2
    nb = width // unit
    grid = tile // unit
    pairs = [(a, b) for a in range(nb) for b in range(a, nb)]
    upper = len(pairs)
    chunk = tile // CHUNKS
    ablocks = order // AB

    r = lax.axis_index("row")
    c = lax.axis_index("col")
    q, core = lax.div(c, 2), lax.rem(c, 2)
    chips = cols // 2
    q0, k0 = lax.div(r, 2), lax.rem(r, 2)
    pa = lax.rem(r, 2)
    pb = 1 - pa
    mate = r + 1 - 2 * pa
    on_line = core == k0
    diag = (q == q0) & on_line
    has_up = on_line & (q >= q0) & (q + 1 < chips)
    has_dn = on_line & (q <= q0) & (q > 0)
    hops = jnp.where(q >= q0, q - q0, q0 - q) + jnp.where(on_line, 0, 1)

    def load_a(s, i):
        return pltpu.make_async_copy(
            inv_hbm.at[0, s, pl.ds(i * AB, AB), pl.ds(i * AB, order - i * AB)],
            a_buf.at[s, pl.ds(i * AB, AB), pl.ds(i * AB, order - i * AB)],
            a_sem.at[s, i])

    def load_m(s):
        return pltpu.make_async_copy(cpl_hbm.at[0, s], m_buf.at[s], m_sem.at[s])

    load_slab = pltpu.make_async_copy(slab_hbm, slab, s_sem)
    for s in range(subs):
        load_m(s).start()
        for i in range(ablocks):
            load_a(s, i).start()
    load_slab.start()

    barrier = pltpu.get_barrier_semaphore()
    for t in range(rows):
        @pl.when(t != r)
        def _():
            pl.semaphore_signal(barrier, inc=1, device_id=(t, c), device_id_type=MESH)
    pl.semaphore_signal(barrier, inc=1, device_id=(r, c + 1 - 2 * core), device_id_type=MESH)

    @pl.when(q + 1 < chips)
    def _():
        pl.semaphore_signal(barrier, inc=1, device_id=(r, c + 2), device_id_type=MESH)

    @pl.when(q > 0)
    def _():
        pl.semaphore_signal(barrier, inc=1, device_id=(r, c - 2), device_id_type=MESH)

    for k in range(pivots.shape[0]):
        piv[pl.ds(k * 128, 128), :] = jnp.transpose(
            jnp.broadcast_to(pivots[pl.ds(k, 1), :], (128, 128)))
    for t in range(rows):
        recv[t, nb * nb] = jnp.zeros((unit, unit), BF16)

    for s in range(subs):
        load_m(s).wait()
        live = lax.broadcasted_iota(jnp.int32, (order, width), 0) < orders[0, s]
        mm[...] = jnp.where(live, m_buf[s], jnp.zeros((order, width), BF16))
        for i in range(ablocks):
            load_a(s, i).wait()
            lo = i * AB
            half = a_buf[s, lo:lo + AB, lo:lo + AB] * jnp.asarray(0.5, BF16)
            part = jnp.dot(half, mm[lo:lo + AB], preferred_element_type=F32)
            if i + 1 < ablocks:
                part = part + jnp.dot(a_buf[s, lo:lo + AB, lo + AB:], mm[lo + AB:],
                                      preferred_element_type=F32)
            sol[lo:lo + AB] = part.astype(BF16)
        half_tile = contract0(mm[...], sol[...])
        whole_tile = (half_tile + jnp.transpose(half_tile)).astype(BF16)
        for k, (a, b) in enumerate(pairs):
            tiles[s, k] = whole_tile[a * unit:(a + 1) * unit, b * unit:(b + 1) * unit]

    neighbours = rows + jnp.where(q + 1 < chips, 1, 0) + jnp.where(q > 0, 1, 0)
    pl.semaphore_wait(barrier, neighbours)

    def pick(src, dst):
        found, which = jnp.int32(0), jnp.int32(0)
        for s in range(subs):
            hit = owners[src, s, 0] == dst
            found, which = jnp.where(hit, 1, found), jnp.where(hit, s, which)
        return found, which

    def tile_copy(t, src_row):
        return pltpu.make_async_remote_copy(
            src_ref=send.at[t], dst_ref=recv.at[src_row, pl.ds(0, upper)],
            send_sem=t_send.at[t], recv_sem=t_recv.at[src_row],
            device_id=(t, c), device_id_type=MESH)

    for t in range(rows):
        _, which = pick(r, t)
        value = tiles[which]

        @pl.when(t != r)
        def _():
            send[t] = value
            tile_copy(t, r).start()

        @pl.when(t == r)
        def _():
            recv[t, pl.ds(0, upper)] = value

    def part(ref, p, j):
        return ref.at[p, pl.ds(pl.multiple_of(j * chunk, chunk), chunk)]

    def panel_copy(j, target, sems):
        return pltpu.make_async_remote_copy(
            src_ref=part(panel, pa, j), dst_ref=part(panel, pa, j),
            send_sem=sems.at[j], recv_sem=g_recv.at[pa, j],
            device_id=(target, c), device_id_type=MESH)

    def panel_got(p, j):
        pltpu.make_async_remote_copy(
            src_ref=part(panel, p, j), dst_ref=part(panel, p, j),
            send_sem=ax_send.at[j], recv_sem=g_recv.at[p, j],
            device_id=(mate, c), device_id_type=MESH).wait_recv()

    def send_panel(j):
        @pl.when(r + 2 < rows)
        def _():
            panel_copy(j, r + 2, ay_send).start()
        panel_copy(j, mate, ax_send).start()

    def left_copy(src, p, j, target, sems):
        return pltpu.make_async_remote_copy(
            src_ref=part(src, p, j), dst_ref=part(left, p, j),
            send_sem=sems.at[p, j], recv_sem=l_recv.at[p, j],
            device_id=(r, target), device_id_type=MESH)

    def forward(src, p, j):
        @pl.when(has_up)
        def _():
            left_copy(src, p, j, c + 2, up_send).start()

        @pl.when(has_dn)
        def _():
            left_copy(src, p, j, c - 2, dn_send).start()
        left_copy(src, p, j, c + 1 - 2 * core, core_send).start()

    load_slab.wait()
    places = []
    for t in range(rows):
        found, which = pick(t, r)
        places.append((found, offsets[t, which, 0], offsets[t, which, 1]))

        @pl.when(t != r)
        def _():
            tile_copy(t, t).wait_recv()
    low = [(a, b) for a in range(nb) for b in range(a)]
    for t in range(rows):
        for k, (a, b) in enumerate(low):
            mirror = recv[t, pairs.index((b, a))].astype(F32)
            recv[t, upper + k] = jnp.transpose(mirror).astype(BF16)
    slots = {pair: k for k, pair in enumerate(pairs + low)}
    for i in range(grid):
        for j in range(grid):
            block = slab[i * unit:(i + 1) * unit, j * unit:(j + 1) * unit]
            total = jnp.zeros((unit, unit), F32)
            for t in range(rows):
                found, at_row, at_col = places[t]
                slot = jnp.int32(nb * nb)
                for (a, b), k in slots.items():
                    here = (found > 0) & (at_row + a == i) & (at_col + b == j)
                    slot = jnp.where(here, k, slot)
                total = total + recv[t, slot].astype(F32)
            out[i * unit:(i + 1) * unit, j * unit:(j + 1) * unit] = block - total

        @pl.when(r < 2)
        def _():
            span = slice(i * unit, (i + 1) * unit)
            panel[pa, span] = out[span, :].astype(BF16)
            for j in range(i * unit // chunk, (i + 1) * unit // chunk):
                send_panel(j)

    per_group = CHUNKS // GROUPS
    depth = per_group * chunk
    lanes = tile // 128

    def step(n, carry):
        @pl.when(n < CHUNKS)
        def _():
            @pl.when(r >= 2)
            def _():
                panel_got(pa, n)
                send_panel(n)

            @pl.when(diag)
            def _():
                forward(panel, pa, n)
            panel_got(pb, n)

            @pl.when(diag)
            def _():
                forward(panel, pb, n)
        j = n - hops

        @pl.when(j >= 0)
        def _():
            for p in (pa, pb):
                @pl.when(jnp.logical_not(diag))
                def _():
                    left_copy(left, p, j, c + 1 - 2 * core, core_send).wait_recv()

                    @pl.when(on_line)
                    def _():
                        forward(left, p, j)

                @pl.when(diag)
                def _():
                    at = pl.ds(pl.multiple_of(j * chunk, chunk), chunk)
                    left[p, at] = panel[p, at]

            @pl.when(lax.rem(j, per_group) == per_group - 1)
            def _():
                first = pl.multiple_of((j - (per_group - 1)) * chunk, depth)
                total = jnp.zeros((tile, tile), F32)
                for p in range(2):
                    pivot = piv[pl.ds(pl.multiple_of(p * tile + first, depth), depth), :]
                    raw = left[p, pl.ds(first, depth)].astype(F32)
                    factor = (raw / jnp.concatenate([pivot] * lanes, axis=1)).astype(BF16)
                    total = total + contract0(factor, panel[p, pl.ds(first, depth)])
                out[...] = out[...] - total
        return carry

    lax.fori_loop(0, CHUNKS + hops, step, 0)

    for t in range(rows):
        @pl.when(t != r)
        def _():
            tile_copy(t, r).wait_send()

    def drain(j, carry):
        @pl.when(r + 2 < rows)
        def _():
            panel_copy(j, r + 2, ay_send).wait_send()
        panel_copy(j, mate, ax_send).wait_send()

        @pl.when(on_line)
        def _():
            for p in range(2):
                @pl.when(has_up)
                def _():
                    left_copy(left, p, j, c + 2, up_send).wait_send()

                @pl.when(has_dn)
                def _():
                    left_copy(left, p, j, c - 2, dn_send).wait_send()
                left_copy(left, p, j, c + 1 - 2 * core, core_send).wait_send()
        return carry

    lax.fori_loop(0, CHUNKS, drain, 0)


def body(rows, cols, inverses, coupling, orders, owners, offsets, dense_slab, pivots):
    subs, order = inverses.shape[1], inverses.shape[2]
    width, tile = coupling.shape[3], dense_slab.shape[0]
    unit = (tile - width) // 2
    nb = width // unit
    upper = nb * (nb + 1) // 2
    panel_width = pivots.shape[0]
    assert panel_width == 2 * tile and rows % 2 == 0 and cols % 2 == 0
    dma = pltpu.SemaphoreType.DMA
    hbm = pl.BlockSpec(memory_space=pl.ANY)
    smem = pl.BlockSpec(memory_space=pltpu.SMEM)
    vmem = pl.BlockSpec(memory_space=pltpu.VMEM)
    return pl.pallas_call(
        functools.partial(kernel, (rows, cols, subs, order, width, tile)),
        out_shape=jax.ShapeDtypeStruct((tile, tile), F32),
        in_specs=[hbm, hbm, smem, smem, smem, hbm, vmem],
        out_specs=vmem,
        scratch_shapes=[
            pltpu.VMEM((subs, order, order), BF16),
            pltpu.VMEM((subs, order, width), BF16),
            pltpu.VMEM((tile, tile), F32),
            pltpu.VMEM((order, width), BF16),
            pltpu.VMEM((order, width), BF16),
            pltpu.VMEM((subs, upper, unit, unit), BF16),
            pltpu.VMEM((rows, upper, unit, unit), BF16),
            pltpu.VMEM((rows, nb * nb + 1, unit, unit), BF16),
            pltpu.VMEM((2, tile, tile), BF16),
            pltpu.VMEM((2, tile, tile), BF16),
            pltpu.VMEM((panel_width, 128), F32),
            dma((subs, order // AB)), dma((subs,)), dma(()),
            dma((rows,)), dma((rows,)),
            dma((CHUNKS,)), dma((CHUNKS,)), dma((2, CHUNKS)),
            dma((2, CHUNKS)), dma((2, CHUNKS)), dma((2, CHUNKS)), dma((2, CHUNKS)),
        ],
        compiler_params=pltpu.CompilerParams(collective_id=0, has_side_effects=True),
    )(inverses, coupling, orders, owners, offsets, dense_slab, pivots.reshape(-1, 128))


def solution(mesh):
    placed = (
        P("row", "col", None, None),
        P("row", "col", None, None),
        P("row", "col"),
        P(None, "col", None),
        P(None, "col", None),
        P("row", "col"),
        P(),
    )
    return jax.shard_map(
        functools.partial(body, mesh.shape["row"], mesh.shape["col"]),
        mesh=mesh, in_specs=placed, out_specs=P("row", "col"), check_vma=False)
```

```python
import functools
import jax
import jax.numpy as jnp
from jax import lax
from jax.experimental import pallas as pl
from jax.experimental.pallas import tpu as pltpu
from jax.sharding import PartitionSpec as P

MESH = pl.DeviceIdType.MESH
BF16 = jnp.bfloat16
F32 = jnp.float32
CHUNKS = 8
AB = 256


def contract0(a, b):
    return lax.dot_general(a, b, (((0,), (0,)), ((), ())), preferred_element_type=F32)


def kernel(
    dims,
    inv_hbm, cpl_hbm, orders, owners, offsets, slab_hbm, pivots,
    out,
    a_buf, m_buf, slab, mm, sol, tiles, send, recv, placed, panel, left, piv,
    a_sem, m_sem, s_sem, t_send, t_recv, ax_send, ay_send, g_recv,
    up_send, dn_send, core_send, l_recv,
):
    rows, cols, subs, order, width, tile = dims
    unit = (tile - width) // 2
    nb = width // unit
    grid = tile // unit
    pairs = [(a, b) for a in range(nb) for b in range(a, nb)]
    chunk = tile // CHUNKS
    ablocks = order // AB

    r = lax.axis_index("row")
    c = lax.axis_index("col")
    q, core = lax.div(c, 2), lax.rem(c, 2)
    chips = cols // 2
    q0, k0 = lax.div(r, 2), lax.rem(r, 2)
    pa = lax.rem(r, 2)
    pb = 1 - pa
    mate = r + 1 - 2 * pa
    on_line = core == k0
    diag = (q == q0) & on_line
    has_up = on_line & (q >= q0) & (q + 1 < chips)
    has_dn = on_line & (q <= q0) & (q > 0)
    chip_hops = jnp.where(q >= q0, q - q0, q0 - q)

    def load_a(s, i):
        return pltpu.make_async_copy(
            inv_hbm.at[0, s, pl.ds(i * AB, AB), pl.ds(i * AB, order - i * AB)],
            a_buf.at[s, pl.ds(i * AB, AB), pl.ds(i * AB, order - i * AB)],
            a_sem.at[s, i])

    def load_m(s):
        return pltpu.make_async_copy(cpl_hbm.at[0, s], m_buf.at[s], m_sem.at[s])

    load_slab = pltpu.make_async_copy(slab_hbm, slab, s_sem)
    for s in range(subs):
        load_m(s).start()
        for i in range(ablocks):
            load_a(s, i).start()
    load_slab.start()

    barrier = pltpu.get_barrier_semaphore()
    for t in range(rows):
        @pl.when(t != r)
        def _():
            pl.semaphore_signal(barrier, inc=1, device_id=(t, c), device_id_type=MESH)
    pl.semaphore_signal(barrier, inc=1, device_id=(r, c + 1 - 2 * core), device_id_type=MESH)

    @pl.when(q + 1 < chips)
    def _():
        pl.semaphore_signal(barrier, inc=1, device_id=(r, c + 2), device_id_type=MESH)

    @pl.when(q > 0)
    def _():
        pl.semaphore_signal(barrier, inc=1, device_id=(r, c - 2), device_id_type=MESH)

    for k in range(pivots.shape[0]):
        piv[pl.ds(k * 128, 128), :] = jnp.transpose(
            jnp.broadcast_to(pivots[pl.ds(k, 1), :], (128, 128)))
    for t in range(rows):
        for k in range(nb + 1):
            placed[t, k * (nb + 1) + nb] = jnp.zeros((unit, unit), BF16)
            placed[t, nb * (nb + 1) + k] = jnp.zeros((unit, unit), BF16)

    for s in range(subs):
        load_m(s).wait()
        live = lax.broadcasted_iota(jnp.int32, (order, width), 0) < orders[0, s]
        mm[...] = jnp.where(live, m_buf[s], jnp.zeros((order, width), BF16))
        for i in range(ablocks):
            load_a(s, i).wait()
            lo = i * AB
            half = a_buf[s, lo:lo + AB, lo:lo + AB] * jnp.asarray(0.5, BF16)
            part = jnp.dot(half, mm[lo:lo + AB], preferred_element_type=F32)
            if i + 1 < ablocks:
                part = part + jnp.dot(a_buf[s, lo:lo + AB, lo + AB:], mm[lo + AB:],
                                      preferred_element_type=F32)
            sol[lo:lo + AB] = part.astype(BF16)
        half_tile = contract0(mm[...], sol[...])
        whole_tile = (half_tile + jnp.transpose(half_tile)).astype(BF16)
        for k, (a, b) in enumerate(pairs):
            tiles[s, k] = whole_tile[a * unit:(a + 1) * unit, b * unit:(b + 1) * unit]

    neighbours = rows + jnp.where(q + 1 < chips, 1, 0) + jnp.where(q > 0, 1, 0)
    pl.semaphore_wait(barrier, neighbours)

    def pick(src, dst):
        found, which = jnp.int32(0), jnp.int32(0)
        for s in range(subs):
            hit = owners[src, 0, s] == dst
            found, which = jnp.where(hit, 1, found), jnp.where(hit, s, which)
        return found, which

    def tile_copy(t, src_row):
        return pltpu.make_async_remote_copy(
            src_ref=send.at[t], dst_ref=recv.at[src_row],
            send_sem=t_send.at[t], recv_sem=t_recv.at[src_row],
            device_id=(t, c), device_id_type=MESH)

    for t in range(rows):
        _, which = pick(r, t)
        value = tiles[which]

        @pl.when(t != r)
        def _():
            send[t] = value
            tile_copy(t, r).start()

        @pl.when(t == r)
        def _():
            recv[t] = value

    def part(ref, p, j):
        return ref.at[p, pl.ds(pl.multiple_of(j * chunk, chunk), chunk)]

    def panel_copy(j, target, sems):
        return pltpu.make_async_remote_copy(
            src_ref=part(panel, pa, j), dst_ref=part(panel, pa, j),
            send_sem=sems.at[j], recv_sem=g_recv.at[pa, j],
            device_id=(target, c), device_id_type=MESH)

    def panel_got(p, j):
        pltpu.make_async_remote_copy(
            src_ref=part(panel, p, j), dst_ref=part(panel, p, j),
            send_sem=ax_send.at[j], recv_sem=g_recv.at[p, j],
            device_id=(mate, c), device_id_type=MESH).wait_recv()

    def send_panel(j):
        @pl.when(r + 2 < rows)
        def _():
            panel_copy(j, r + 2, ay_send).start()
        panel_copy(j, mate, ax_send).start()

    def left_copy(src, p, j, target, sems):
        return pltpu.make_async_remote_copy(
            src_ref=part(src, p, j), dst_ref=part(left, p, j),
            send_sem=sems.at[p, j], recv_sem=l_recv.at[p, j],
            device_id=(r, target), device_id_type=MESH)

    def forward(src, p, j):
        @pl.when(has_up)
        def _():
            left_copy(src, p, j, c + 2, up_send).start()

        @pl.when(has_dn)
        def _():
            left_copy(src, p, j, c - 2, dn_send).start()
        left_copy(src, p, j, c + 1 - 2 * core, core_send).start()

    load_slab.wait()
    places = []
    side = nb + 1
    for t in range(rows):
        found, which = pick(t, r)
        at_row, at_col = offsets[t, 0, which], offsets[t, 1, which]
        spots = []
        for start in (at_row, at_col):
            inside = [(found > 0) & (k - start >= 0) & (k - start < nb) for k in range(grid)]
            spots.append([jnp.where(ok, k - start, nb) for k, ok in enumerate(inside)])
        places.append(([side * a for a in spots[0]], spots[1]))

        @pl.when(t != r)
        def _():
            tile_copy(t, t).wait_recv()
    for t in range(rows):
        for k, (a, b) in enumerate(pairs):
            value = recv[t, k]
            placed[t, a * side + b] = value
            if a != b:
                placed[t, b * side + a] = jnp.transpose(value.astype(F32)).astype(BF16)
    for i in range(grid):
        for j in range(grid):
            total = slab[i * unit:(i + 1) * unit, j * unit:(j + 1) * unit]
            for t in range(rows):
                total = total - placed[t, places[t][0][i] + places[t][1][j]].astype(F32)
            out[i * unit:(i + 1) * unit, j * unit:(j + 1) * unit] = total

        @pl.when(r < 2)
        def _():
            span = slice(i * unit, (i + 1) * unit)
            panel[pa, span] = out[span, :].astype(BF16)
            for j in range(i * unit // chunk, (i + 1) * unit // chunk):
                send_panel(j)

    lanes = tile // 128
    late = jnp.where(r >= 2, 2, 0)
    first_left = jnp.where(diag, 0, lax.div(5 * chip_hops, 4) + jnp.where(on_line, 0, 1)
                           + jnp.where(r >= 2, 1, 0))

    def step(n, carry):
        @pl.when((n < CHUNKS) & (r >= 2))
        def _():
            panel_got(pa, n)
            send_panel(n)

        def own(p, j):
            @pl.when(diag)
            def _():
                forward(panel, p, j)
                at = pl.ds(pl.multiple_of(j * chunk, chunk), chunk)
                left[p, at] = panel[p, at]

        def other(p, j):
            @pl.when((j >= 0) & (j < CHUNKS) & jnp.logical_not(diag))
            def _():
                left_copy(left, p, j, c + 1 - 2 * core, core_send).wait_recv()

                @pl.when(on_line)
                def _():
                    forward(left, p, j)

        @pl.when(n < CHUNKS)
        def _():
            own(pa, n)
        m = n - late

        @pl.when((m >= 0) & (m < CHUNKS))
        def _():
            panel_got(pb, m)
            own(pb, m)
        other(pa, n - first_left)
        j = m - first_left
        other(pb, j)

        @pl.when(j >= 0)
        def _():
            at = pl.ds(pl.multiple_of(j * chunk, chunk), chunk)
            factors, rights = [], []
            for p in range(2):
                pivot = piv[pl.ds(pl.multiple_of(p * tile + j * chunk, chunk), chunk), :]
                raw = left[p, at].astype(F32)
                factors.append((raw / jnp.concatenate([pivot] * lanes, axis=1)).astype(BF16))
                rights.append(panel[p, at])
            factor = jnp.concatenate(factors, axis=0)
            out[...] = out[...] - contract0(factor, jnp.concatenate(rights, axis=0))
        return carry

    lax.fori_loop(0, CHUNKS + first_left + late, step, 0)

    for t in range(rows):
        @pl.when(t != r)
        def _():
            tile_copy(t, r).wait_send()

    def drain(j, carry):
        @pl.when(r + 2 < rows)
        def _():
            panel_copy(j, r + 2, ay_send).wait_send()
        panel_copy(j, mate, ax_send).wait_send()

        @pl.when(on_line)
        def _():
            for p in range(2):
                @pl.when(has_up)
                def _():
                    left_copy(left, p, j, c + 2, up_send).wait_send()

                @pl.when(has_dn)
                def _():
                    left_copy(left, p, j, c - 2, dn_send).wait_send()
                left_copy(left, p, j, c + 1 - 2 * core, core_send).wait_send()
        return carry

    lax.fori_loop(0, CHUNKS, drain, 0)


def body(rows, cols, inverses, coupling, orders, owners, offsets, dense_slab, pivots):
    subs, order = inverses.shape[1], inverses.shape[2]
    width, tile = coupling.shape[3], dense_slab.shape[0]
    unit = (tile - width) // 2
    nb = width // unit
    upper = nb * (nb + 1) // 2
    panel_width = pivots.shape[0]
    assert panel_width == 2 * tile and rows % 2 == 0 and cols % 2 == 0
    dma = pltpu.SemaphoreType.DMA
    hbm = pl.BlockSpec(memory_space=pl.ANY)
    smem = pl.BlockSpec(memory_space=pltpu.SMEM)
    vmem = pl.BlockSpec(memory_space=pltpu.VMEM)
    return pl.pallas_call(
        functools.partial(kernel, (rows, cols, subs, order, width, tile)),
        out_shape=pltpu.VMEM((tile, tile), F32),
        in_specs=[hbm, hbm, smem, smem, smem, hbm, vmem],
        out_specs=vmem,
        scratch_shapes=[
            pltpu.VMEM((subs, order, order), BF16),
            pltpu.VMEM((subs, order, width), BF16),
            pltpu.VMEM((tile, tile), F32),
            pltpu.VMEM((order, width), BF16),
            pltpu.VMEM((order, width), BF16),
            pltpu.VMEM((subs, upper, unit, unit), BF16),
            pltpu.VMEM((rows, upper, unit, unit), BF16),
            pltpu.VMEM((rows, upper, unit, unit), BF16),
            pltpu.VMEM((rows, (nb + 1) * (nb + 1), unit, unit), BF16),
            pltpu.VMEM((2, tile, tile), BF16),
            pltpu.VMEM((2, tile, tile), BF16),
            pltpu.VMEM((panel_width, 128), F32),
            dma((subs, order // AB)), dma((subs,)), dma(()),
            dma((rows,)), dma((rows,)),
            dma((CHUNKS,)), dma((CHUNKS,)), dma((2, CHUNKS)),
            dma((2, CHUNKS)), dma((2, CHUNKS)), dma((2, CHUNKS)), dma((2, CHUNKS)),
        ],
        compiler_params=pltpu.CompilerParams(collective_id=0, has_side_effects=True),
    )(inverses, coupling, orders, jnp.transpose(owners, (0, 2, 1)),
      jnp.transpose(offsets, (0, 2, 1)), dense_slab, pivots.reshape(-1, 128))


def solution(mesh):
    placed = (
        P("row", "col", None, None),
        P("row", "col", None, None),
        P("row", "col"),
        P(None, "col", None),
        P(None, "col", None),
        P("row", "col"),
        P(),
    )
    return jax.shard_map(
        functools.partial(body, mesh.shape["row"], mesh.shape["col"]),
        mesh=mesh, in_specs=placed, out_specs=P("row", "col"), check_vma=False)
```

```python
import functools
import jax
import jax.numpy as jnp
from jax import lax
from jax.experimental import pallas as pl
from jax.experimental.pallas import tpu as pltpu
from jax.sharding import PartitionSpec as P

MESH = pl.DeviceIdType.MESH
BF16 = jnp.bfloat16
F32 = jnp.float32
CHUNKS = 16
MERGE = 2
AB = 256


def contract0(a, b):
    return lax.dot_general(a, b, (((0,), (0,)), ((), ())), preferred_element_type=F32)


def kernel(
    dims,
    inv_hbm, cpl_hbm, orders, owners, offsets, slab_hbm, pivots,
    out,
    a_buf, m_buf, slab, mm, sol, tiles, send, recv, placed, panel, left, piv,
    a_sem, m_sem, s_sem, t_send, t_recv, ax_send, ay_send, g_recv,
    up_send, dn_send, core_send, l_recv,
):
    rows, cols, subs, order, width, tile = dims
    unit = (tile - width) // 2
    nb = width // unit
    grid = tile // unit
    pairs = [(a, b) for a in range(nb) for b in range(a, nb)]
    chunk = tile // CHUNKS
    ablocks = order // AB

    r = lax.axis_index("row")
    c = lax.axis_index("col")
    q, core = lax.div(c, 2), lax.rem(c, 2)
    chips = cols // 2
    q0, k0 = lax.div(r, 2), lax.rem(r, 2)
    pa = lax.rem(r, 2)
    pb = 1 - pa
    mate = r + 1 - 2 * pa
    on_line = core == k0
    diag = (q == q0) & on_line
    has_up = on_line & (q >= q0) & (q + 1 < chips)
    has_dn = on_line & (q <= q0) & (q > 0)
    chip_hops = jnp.where(q >= q0, q - q0, q0 - q)

    def load_a(s, i):
        return pltpu.make_async_copy(
            inv_hbm.at[0, s, pl.ds(i * AB, AB), pl.ds(i * AB, order - i * AB)],
            a_buf.at[s, pl.ds(i * AB, AB), pl.ds(i * AB, order - i * AB)],
            a_sem.at[s, i])

    def load_m(s):
        return pltpu.make_async_copy(cpl_hbm.at[0, s], m_buf.at[s], m_sem.at[s])

    load_slab = pltpu.make_async_copy(slab_hbm, slab, s_sem)
    for s in range(subs):
        load_m(s).start()
        for i in range(ablocks):
            load_a(s, i).start()
    load_slab.start()

    barrier = pltpu.get_barrier_semaphore()
    for t in range(rows):
        @pl.when(t != r)
        def _():
            pl.semaphore_signal(barrier, inc=1, device_id=(t, c), device_id_type=MESH)
    pl.semaphore_signal(barrier, inc=1, device_id=(r, c + 1 - 2 * core), device_id_type=MESH)

    @pl.when(q + 1 < chips)
    def _():
        pl.semaphore_signal(barrier, inc=1, device_id=(r, c + 2), device_id_type=MESH)

    @pl.when(q > 0)
    def _():
        pl.semaphore_signal(barrier, inc=1, device_id=(r, c - 2), device_id_type=MESH)

    for k in range(pivots.shape[0]):
        piv[pl.ds(k * 128, 128), :] = jnp.transpose(
            jnp.broadcast_to(pivots[pl.ds(k, 1), :], (128, 128)))
    for t in range(rows):
        for k in range(nb + 1):
            placed[t, k * (nb + 1) + nb] = jnp.zeros((unit, unit), BF16)
            placed[t, nb * (nb + 1) + k] = jnp.zeros((unit, unit), BF16)

    for s in range(subs):
        load_m(s).wait()
        live = lax.broadcasted_iota(jnp.int32, (order, width), 0) < orders[0, s]
        mm[...] = jnp.where(live, m_buf[s], jnp.zeros((order, width), BF16))
        for i in range(ablocks):
            load_a(s, i).wait()
            lo = i * AB
            half = a_buf[s, lo:lo + AB, lo:lo + AB] * jnp.asarray(0.5, BF16)
            part = jnp.dot(half, mm[lo:lo + AB], preferred_element_type=F32)
            if i + 1 < ablocks:
                part = part + jnp.dot(a_buf[s, lo:lo + AB, lo + AB:], mm[lo + AB:],
                                      preferred_element_type=F32)
            sol[lo:lo + AB] = part.astype(BF16)
        half_tile = contract0(mm[...], sol[...])
        whole_tile = (half_tile + jnp.transpose(half_tile)).astype(BF16)
        for k, (a, b) in enumerate(pairs):
            tiles[s, k] = whole_tile[a * unit:(a + 1) * unit, b * unit:(b + 1) * unit]

    neighbours = rows + jnp.where(q + 1 < chips, 1, 0) + jnp.where(q > 0, 1, 0)
    pl.semaphore_wait(barrier, neighbours)

    def pick(src, dst):
        found, which = jnp.int32(0), jnp.int32(0)
        for s in range(subs):
            hit = owners[src, 0, s] == dst
            found, which = jnp.where(hit, 1, found), jnp.where(hit, s, which)
        return found, which

    def tile_copy(t, src_row):
        return pltpu.make_async_remote_copy(
            src_ref=send.at[t], dst_ref=recv.at[src_row],
            send_sem=t_send.at[t], recv_sem=t_recv.at[src_row],
            device_id=(t, c), device_id_type=MESH)

    for t in range(rows):
        _, which = pick(r, t)
        value = tiles[which]

        @pl.when(t != r)
        def _():
            send[t] = value
            tile_copy(t, r).start()

        @pl.when(t == r)
        def _():
            recv[t] = value

    def part(ref, p, j):
        return ref.at[p, pl.ds(pl.multiple_of(j * chunk, chunk), chunk)]

    def panel_copy(j, target, sems):
        return pltpu.make_async_remote_copy(
            src_ref=part(panel, pa, j), dst_ref=part(panel, pa, j),
            send_sem=sems.at[j], recv_sem=g_recv.at[pa, j],
            device_id=(target, c), device_id_type=MESH)

    def panel_got(p, j):
        pltpu.make_async_remote_copy(
            src_ref=part(panel, p, j), dst_ref=part(panel, p, j),
            send_sem=ax_send.at[j], recv_sem=g_recv.at[p, j],
            device_id=(mate, c), device_id_type=MESH).wait_recv()

    def send_panel(j):
        @pl.when(r + 2 < rows)
        def _():
            panel_copy(j, r + 2, ay_send).start()
        panel_copy(j, mate, ax_send).start()

    def left_copy(src, p, j, target, sems):
        return pltpu.make_async_remote_copy(
            src_ref=part(src, p, j), dst_ref=part(left, p, j),
            send_sem=sems.at[p, j], recv_sem=l_recv.at[p, j],
            device_id=(r, target), device_id_type=MESH)

    def forward(src, p, j):
        @pl.when(has_up)
        def _():
            left_copy(src, p, j, c + 2, up_send).start()

        @pl.when(has_dn)
        def _():
            left_copy(src, p, j, c - 2, dn_send).start()
        left_copy(src, p, j, c + 1 - 2 * core, core_send).start()

    load_slab.wait()
    places = []
    side = nb + 1
    for t in range(rows):
        found, which = pick(t, r)
        at_row, at_col = offsets[t, 0, which], offsets[t, 1, which]
        spots = []
        for start in (at_row, at_col):
            inside = [(found > 0) & (k - start >= 0) & (k - start < nb) for k in range(grid)]
            spots.append([jnp.where(ok, k - start, nb) for k, ok in enumerate(inside)])
        places.append(([side * a for a in spots[0]], spots[1]))

        @pl.when(t != r)
        def _():
            tile_copy(t, t).wait_recv()
    for t in range(rows):
        for k, (a, b) in enumerate(pairs):
            value = recv[t, k]
            placed[t, a * side + b] = value
            if a != b:
                placed[t, b * side + a] = jnp.transpose(value.astype(F32)).astype(BF16)
    for i in range(grid):
        for j in range(grid):
            total = slab[i * unit:(i + 1) * unit, j * unit:(j + 1) * unit]
            for t in range(rows):
                total = total - placed[t, places[t][0][i] + places[t][1][j]].astype(F32)
            out[i * unit:(i + 1) * unit, j * unit:(j + 1) * unit] = total

        @pl.when(r < 2)
        def _():
            span = slice(i * unit, (i + 1) * unit)
            panel[pa, span] = out[span, :].astype(BF16)
            for j in range(i * unit // chunk, (i + 1) * unit // chunk):
                send_panel(j)

    lanes = tile // 128
    late = 3
    first_left = jnp.where(diag, 0, 2 * chip_hops + jnp.where(on_line, 0, 1))

    def step(n, carry):
        @pl.when((n < CHUNKS) & (r >= 2))
        def _():
            panel_got(pa, n)
            send_panel(n)

        def own(p, j):
            @pl.when(diag)
            def _():
                forward(panel, p, j)
                at = pl.ds(pl.multiple_of(j * chunk, chunk), chunk)
                left[p, at] = panel[p, at]

        def other(p, j):
            @pl.when((j >= 0) & (j < CHUNKS) & jnp.logical_not(diag))
            def _():
                left_copy(left, p, j, c + 1 - 2 * core, core_send).wait_recv()

                @pl.when(on_line)
                def _():
                    forward(left, p, j)

        @pl.when(n < CHUNKS)
        def _():
            own(pa, n)
        m = n - late

        @pl.when((m >= 0) & (m < CHUNKS) & diag)
        def _():
            panel_got(pb, m)
            own(pb, m)
        other(pa, n - first_left)
        j = m - first_left
        other(pb, j)

        @pl.when((j >= 0) & jnp.logical_not(diag))
        def _():
            panel_got(pb, j)

        @pl.when((j >= 0) & (lax.rem(j, MERGE) == MERGE - 1))
        def _():
            first = pl.multiple_of((j - (MERGE - 1)) * chunk, MERGE * chunk)
            at = pl.ds(first, MERGE * chunk)
            factors, rights = [], []
            for p in range(2):
                pivot = piv[pl.ds(pl.multiple_of(p * tile + first, chunk), MERGE * chunk), :]
                raw = left[p, at].astype(F32)
                factors.append((raw / jnp.concatenate([pivot] * lanes, axis=1)).astype(BF16))
                rights.append(panel[p, at])
            factor = jnp.concatenate(factors, axis=0)
            out[...] = out[...] - contract0(factor, jnp.concatenate(rights, axis=0))
        return carry

    lax.fori_loop(0, CHUNKS + first_left + late, step, 0)

    for t in range(rows):
        @pl.when(t != r)
        def _():
            tile_copy(t, r).wait_send()

    def drain(j, carry):
        @pl.when(r + 2 < rows)
        def _():
            panel_copy(j, r + 2, ay_send).wait_send()
        panel_copy(j, mate, ax_send).wait_send()

        @pl.when(on_line)
        def _():
            for p in range(2):
                @pl.when(has_up)
                def _():
                    left_copy(left, p, j, c + 2, up_send).wait_send()

                @pl.when(has_dn)
                def _():
                    left_copy(left, p, j, c - 2, dn_send).wait_send()
                left_copy(left, p, j, c + 1 - 2 * core, core_send).wait_send()
        return carry

    lax.fori_loop(0, CHUNKS, drain, 0)


def body(rows, cols, inverses, coupling, orders, owners, offsets, dense_slab, pivots):
    subs, order = inverses.shape[1], inverses.shape[2]
    width, tile = coupling.shape[3], dense_slab.shape[0]
    unit = (tile - width) // 2
    nb = width // unit
    upper = nb * (nb + 1) // 2
    panel_width = pivots.shape[0]
    assert panel_width == 2 * tile and rows % 2 == 0 and cols % 2 == 0
    dma = pltpu.SemaphoreType.DMA
    hbm = pl.BlockSpec(memory_space=pl.ANY)
    smem = pl.BlockSpec(memory_space=pltpu.SMEM)
    vmem = pl.BlockSpec(memory_space=pltpu.VMEM)
    return pl.pallas_call(
        functools.partial(kernel, (rows, cols, subs, order, width, tile)),
        out_shape=pltpu.VMEM((tile, tile), F32),
        in_specs=[hbm, hbm, smem, smem, smem, hbm, vmem],
        out_specs=vmem,
        scratch_shapes=[
            pltpu.VMEM((subs, order, order), BF16),
            pltpu.VMEM((subs, order, width), BF16),
            pltpu.VMEM((tile, tile), F32),
            pltpu.VMEM((order, width), BF16),
            pltpu.VMEM((order, width), BF16),
            pltpu.VMEM((subs, upper, unit, unit), BF16),
            pltpu.VMEM((rows, upper, unit, unit), BF16),
            pltpu.VMEM((rows, upper, unit, unit), BF16),
            pltpu.VMEM((rows, (nb + 1) * (nb + 1), unit, unit), BF16),
            pltpu.VMEM((2, tile, tile), BF16),
            pltpu.VMEM((2, tile, tile), BF16),
            pltpu.VMEM((panel_width, 128), F32),
            dma((subs, order // AB)), dma((subs,)), dma(()),
            dma((rows,)), dma((rows,)),
            dma((CHUNKS,)), dma((CHUNKS,)), dma((2, CHUNKS)),
            dma((2, CHUNKS)), dma((2, CHUNKS)), dma((2, CHUNKS)), dma((2, CHUNKS)),
        ],
        compiler_params=pltpu.CompilerParams(collective_id=0, has_side_effects=True),
    )(inverses, coupling, orders, jnp.transpose(owners, (0, 2, 1)),
      jnp.transpose(offsets, (0, 2, 1)), dense_slab, pivots.reshape(-1, 128))


def solution(mesh):
    placed = (
        P("row", "col", None, None),
        P("row", "col", None, None),
        P("row", "col"),
        P(None, "col", None),
        P(None, "col", None),
        P("row", "col"),
        P(),
    )
    return jax.shard_map(
        functools.partial(body, mesh.shape["row"], mesh.shape["col"]),
        mesh=mesh, in_specs=placed, out_specs=P("row", "col"), check_vma=False)
```

```python
import functools
import jax
import jax.numpy as jnp
from jax import lax
from jax.experimental import pallas as pl
from jax.experimental.pallas import tpu as pltpu
from jax.sharding import PartitionSpec as P

MESH = pl.DeviceIdType.MESH
BF16 = jnp.bfloat16
F32 = jnp.float32
CHUNKS = 16
MERGE = 2
AB = 256


def contract0(a, b):
    return lax.dot_general(a, b, (((0,), (0,)), ((), ())), preferred_element_type=F32)


def kernel(
    dims,
    inv_hbm, cpl_hbm, orders, owners, offsets, slab_hbm, pivots,
    out,
    a_buf, m_buf, slab, mm, sol, tiles, send, recv, placed, panel, left, piv,
    a_sem, m_sem, s_sem, t_send, t_recv, ax_send, ay_send, g_recv,
    up_send, dn_send, core_send, l_recv,
):
    rows, cols, subs, order, width, tile = dims
    unit = (tile - width) // 2
    nb = width // unit
    grid = tile // unit
    pairs = [(a, b) for a in range(nb) for b in range(a, nb)]
    chunk = tile // CHUNKS
    ablocks = order // AB

    r = lax.axis_index("row")
    c = lax.axis_index("col")
    q, core = lax.div(c, 2), lax.rem(c, 2)
    chips = cols // 2
    q0, k0 = lax.div(r, 2), lax.rem(r, 2)
    pa = lax.rem(r, 2)
    pb = 1 - pa
    mate = r + 1 - 2 * pa
    on_line = core == k0
    diag = (q == q0) & on_line
    has_up = on_line & (q >= q0) & (q + 1 < chips)
    has_dn = on_line & (q <= q0) & (q > 0)
    chip_hops = jnp.where(q >= q0, q - q0, q0 - q)

    def load_a(s, i):
        return pltpu.make_async_copy(
            inv_hbm.at[0, s, pl.ds(i * AB, AB), pl.ds(i * AB, order - i * AB)],
            a_buf.at[s, pl.ds(i * AB, AB), pl.ds(i * AB, order - i * AB)],
            a_sem.at[s, i])

    def load_m(s):
        return pltpu.make_async_copy(cpl_hbm.at[0, s], m_buf.at[s], m_sem.at[s])

    load_slab = pltpu.make_async_copy(slab_hbm, slab, s_sem)
    for s in range(subs):
        load_m(s).start()
        for i in range(ablocks):
            load_a(s, i).start()
    load_slab.start()

    barrier = pltpu.get_barrier_semaphore()
    for t in range(rows):
        @pl.when(t != r)
        def _():
            pl.semaphore_signal(barrier, inc=1, device_id=(t, c), device_id_type=MESH)
    pl.semaphore_signal(barrier, inc=1, device_id=(r, c + 1 - 2 * core), device_id_type=MESH)

    @pl.when(q + 1 < chips)
    def _():
        pl.semaphore_signal(barrier, inc=1, device_id=(r, c + 2), device_id_type=MESH)

    @pl.when(q > 0)
    def _():
        pl.semaphore_signal(barrier, inc=1, device_id=(r, c - 2), device_id_type=MESH)

    for k in range(pivots.shape[0]):
        piv[pl.ds(k * 128, 128), :] = jnp.transpose(
            jnp.broadcast_to(pivots[pl.ds(k, 1), :], (128, 128)))
    for t in range(rows):
        for k in range(nb + 1):
            placed[t, k * (nb + 1) + nb] = jnp.zeros((unit, unit), BF16)
            placed[t, nb * (nb + 1) + k] = jnp.zeros((unit, unit), BF16)

    for s in range(subs):
        load_m(s).wait()
        live = lax.broadcasted_iota(jnp.int32, (order, width), 0) < orders[0, s]
        mm[...] = jnp.where(live, m_buf[s], jnp.zeros((order, width), BF16))
        for i in range(ablocks):
            load_a(s, i).wait()
            lo = i * AB
            half = a_buf[s, lo:lo + AB, lo:lo + AB] * jnp.asarray(0.5, BF16)
            part = jnp.dot(half, mm[lo:lo + AB], preferred_element_type=F32)
            if i + 1 < ablocks:
                part = part + jnp.dot(a_buf[s, lo:lo + AB, lo + AB:], mm[lo + AB:],
                                      preferred_element_type=F32)
            sol[lo:lo + AB] = part.astype(BF16)
        half_tile = contract0(mm[...], sol[...])
        whole_tile = (half_tile + jnp.transpose(half_tile)).astype(BF16)
        for k, (a, b) in enumerate(pairs):
            tiles[s, k] = whole_tile[a * unit:(a + 1) * unit, b * unit:(b + 1) * unit]

    neighbours = rows + jnp.where(q + 1 < chips, 1, 0) + jnp.where(q > 0, 1, 0)
    pl.semaphore_wait(barrier, neighbours)

    def pick(src, dst):
        found, which = jnp.int32(0), jnp.int32(0)
        for s in range(subs):
            hit = owners[src, 0, s] == dst
            found, which = jnp.where(hit, 1, found), jnp.where(hit, s, which)
        return found, which

    def tile_copy(t, src_row):
        return pltpu.make_async_remote_copy(
            src_ref=send.at[t], dst_ref=recv.at[src_row],
            send_sem=t_send.at[t], recv_sem=t_recv.at[src_row],
            device_id=(t, c), device_id_type=MESH)

    for t in range(rows):
        _, which = pick(r, t)
        value = tiles[which]

        @pl.when(t != r)
        def _():
            send[t] = value
            tile_copy(t, r).start()

        @pl.when(t == r)
        def _():
            recv[t] = value

    def part(ref, p, j):
        return ref.at[p, pl.ds(pl.multiple_of(j * chunk, chunk), chunk)]

    def panel_copy(j, target, sems):
        return pltpu.make_async_remote_copy(
            src_ref=part(panel, pa, j), dst_ref=part(panel, pa, j),
            send_sem=sems.at[j], recv_sem=g_recv.at[pa, j],
            device_id=(target, c), device_id_type=MESH)

    def panel_got(p, j):
        pltpu.make_async_remote_copy(
            src_ref=part(panel, p, j), dst_ref=part(panel, p, j),
            send_sem=ax_send.at[j], recv_sem=g_recv.at[p, j],
            device_id=(mate, c), device_id_type=MESH).wait_recv()

    def send_panel(j):
        @pl.when(r + 2 < rows)
        def _():
            panel_copy(j, r + 2, ay_send).start()
        panel_copy(j, mate, ax_send).start()

    def left_copy(src, p, j, target, sems):
        return pltpu.make_async_remote_copy(
            src_ref=part(src, p, j), dst_ref=part(left, p, j),
            send_sem=sems.at[p, j], recv_sem=l_recv.at[p, j],
            device_id=(r, target), device_id_type=MESH)

    def forward(src, p, j):
        @pl.when(has_up)
        def _():
            left_copy(src, p, j, c + 2, up_send).start()

        @pl.when(has_dn)
        def _():
            left_copy(src, p, j, c - 2, dn_send).start()
        left_copy(src, p, j, c + 1 - 2 * core, core_send).start()

    load_slab.wait()
    places = []
    side = nb + 1
    for t in range(rows):
        found, which = pick(t, r)
        at_row, at_col = offsets[t, 0, which], offsets[t, 1, which]
        spots = []
        for start in (at_row, at_col):
            inside = [(found > 0) & (k - start >= 0) & (k - start < nb) for k in range(grid)]
            spots.append([jnp.where(ok, k - start, nb) for k, ok in enumerate(inside)])
        places.append(([side * a for a in spots[0]], spots[1]))

        @pl.when(t != r)
        def _():
            tile_copy(t, t).wait_recv()
    for t in range(rows):
        for k, (a, b) in enumerate(pairs):
            value = recv[t, k]
            placed[t, a * side + b] = value
            if a != b:
                placed[t, b * side + a] = jnp.transpose(value.astype(F32)).astype(BF16)
    for i in range(grid):
        for j in range(grid):
            total = slab[i * unit:(i + 1) * unit, j * unit:(j + 1) * unit]
            for t in range(rows):
                total = total - placed[t, places[t][0][i] + places[t][1][j]].astype(F32)
            out[i * unit:(i + 1) * unit, j * unit:(j + 1) * unit] = total

        @pl.when(r < 2)
        def _():
            span = slice(i * unit, (i + 1) * unit)
            panel[pa, span] = out[span, :].astype(BF16)
            for j in range(i * unit // chunk, (i + 1) * unit // chunk):
                send_panel(j)

    lanes = tile // 128
    late = 4
    off_line = jnp.where(on_line, 0, 2)
    first_left = jnp.where(diag | (r < 2), 0, 4 * chip_hops + off_line)

    def step(n, carry):
        @pl.when((n < CHUNKS) & (r >= 2))
        def _():
            panel_got(pa, n)
            send_panel(n)

        def own(p, j):
            @pl.when(diag)
            def _():
                forward(panel, p, j)
                at = pl.ds(pl.multiple_of(j * chunk, chunk), chunk)
                left[p, at] = panel[p, at]

        def other(p, j):
            @pl.when((j >= 0) & (j < CHUNKS) & jnp.logical_not(diag))
            def _():
                left_copy(left, p, j, c + 1 - 2 * core, core_send).wait_recv()

                @pl.when(on_line)
                def _():
                    forward(left, p, j)

        @pl.when(n < CHUNKS)
        def _():
            own(pa, n)
        m = n - late

        @pl.when((m >= 0) & (m < CHUNKS) & diag)
        def _():
            panel_got(pb, m)
            own(pb, m)
        other(pa, n - first_left)
        j = m - first_left
        other(pb, j)

        @pl.when((j >= 0) & jnp.logical_not(diag))
        def _():
            panel_got(pb, j)

        @pl.when((j >= 0) & (lax.rem(j, MERGE) == MERGE - 1))
        def _():
            first = pl.multiple_of((j - (MERGE - 1)) * chunk, MERGE * chunk)
            at = pl.ds(first, MERGE * chunk)
            factors, rights = [], []
            for p in range(2):
                pivot = piv[pl.ds(pl.multiple_of(p * tile + first, chunk), MERGE * chunk), :]
                raw = left[p, at].astype(F32)
                factors.append((raw / jnp.concatenate([pivot] * lanes, axis=1)).astype(BF16))
                rights.append(panel[p, at])
            factor = jnp.concatenate(factors, axis=0)
            out[...] = out[...] - contract0(factor, jnp.concatenate(rights, axis=0))
        return carry

    lax.fori_loop(0, CHUNKS + first_left + late, step, 0)

    for t in range(rows):
        @pl.when(t != r)
        def _():
            tile_copy(t, r).wait_send()

    def drain(j, carry):
        @pl.when(r + 2 < rows)
        def _():
            panel_copy(j, r + 2, ay_send).wait_send()
        panel_copy(j, mate, ax_send).wait_send()

        @pl.when(on_line)
        def _():
            for p in range(2):
                @pl.when(has_up)
                def _():
                    left_copy(left, p, j, c + 2, up_send).wait_send()

                @pl.when(has_dn)
                def _():
                    left_copy(left, p, j, c - 2, dn_send).wait_send()
                left_copy(left, p, j, c + 1 - 2 * core, core_send).wait_send()
        return carry

    lax.fori_loop(0, CHUNKS, drain, 0)


def body(rows, cols, inverses, coupling, orders, owners, offsets, dense_slab, pivots):
    subs, order = inverses.shape[1], inverses.shape[2]
    width, tile = coupling.shape[3], dense_slab.shape[0]
    unit = (tile - width) // 2
    nb = width // unit
    upper = nb * (nb + 1) // 2
    panel_width = pivots.shape[0]
    assert panel_width == 2 * tile and rows % 2 == 0 and cols % 2 == 0
    dma = pltpu.SemaphoreType.DMA
    hbm = pl.BlockSpec(memory_space=pl.ANY)
    smem = pl.BlockSpec(memory_space=pltpu.SMEM)
    vmem = pl.BlockSpec(memory_space=pltpu.VMEM)
    return pl.pallas_call(
        functools.partial(kernel, (rows, cols, subs, order, width, tile)),
        out_shape=pltpu.VMEM((tile, tile), F32),
        in_specs=[hbm, hbm, smem, smem, smem, hbm, vmem],
        out_specs=vmem,
        scratch_shapes=[
            pltpu.VMEM((subs, order, order), BF16),
            pltpu.VMEM((subs, order, width), BF16),
            pltpu.VMEM((tile, tile), F32),
            pltpu.VMEM((order, width), BF16),
            pltpu.VMEM((order, width), BF16),
            pltpu.VMEM((subs, upper, unit, unit), BF16),
            pltpu.VMEM((rows, upper, unit, unit), BF16),
            pltpu.VMEM((rows, upper, unit, unit), BF16),
            pltpu.VMEM((rows, (nb + 1) * (nb + 1), unit, unit), BF16),
            pltpu.VMEM((2, tile, tile), BF16),
            pltpu.VMEM((2, tile, tile), BF16),
            pltpu.VMEM((panel_width, 128), F32),
            dma((subs, order // AB)), dma((subs,)), dma(()),
            dma((rows,)), dma((rows,)),
            dma((CHUNKS,)), dma((CHUNKS,)), dma((2, CHUNKS)),
            dma((2, CHUNKS)), dma((2, CHUNKS)), dma((2, CHUNKS)), dma((2, CHUNKS)),
        ],
        compiler_params=pltpu.CompilerParams(collective_id=0, has_side_effects=True),
    )(inverses, coupling, orders, jnp.transpose(owners, (0, 2, 1)),
      jnp.transpose(offsets, (0, 2, 1)), dense_slab, pivots.reshape(-1, 128))


def solution(mesh):
    placed = (
        P("row", "col", None, None),
        P("row", "col", None, None),
        P("row", "col"),
        P(None, "col", None),
        P(None, "col", None),
        P("row", "col"),
        P(),
    )
    return jax.shard_map(
        functools.partial(body, mesh.shape["row"], mesh.shape["col"]),
        mesh=mesh, in_specs=placed, out_specs=P("row", "col"), check_vma=False)
```

```python
import functools
import jax
import jax.numpy as jnp
from jax import lax
from jax.experimental import pallas as pl
from jax.experimental.pallas import tpu as pltpu
from jax.sharding import PartitionSpec as P

MESH = pl.DeviceIdType.MESH
BF16 = jnp.bfloat16
F32 = jnp.float32
CHUNKS = 16
MERGE = 2
AB = 256


def contract0(a, b):
    return lax.dot_general(a, b, (((0,), (0,)), ((), ())), preferred_element_type=F32)


def kernel(
    dims,
    inv_hbm, cpl_hbm, orders, owners, offsets, slab_hbm, pivots,
    out,
    a_buf, m_buf, slab, mm, sol, send, recv, placed, panel, left, piv,
    a_sem, m_sem, s_sem, t_send, t_recv, ax_send, ay_send, g_recv,
    up_send, dn_send, core_send, l_recv,
):
    rows, cols, subs, order, width, tile = dims
    unit = (tile - width) // 2
    nb = width // unit
    grid = tile // unit
    pairs = [(a, b) for a in range(nb) for b in range(a, nb)]
    chunk = tile // CHUNKS
    ablocks = order // AB

    r = lax.axis_index("row")
    c = lax.axis_index("col")
    q, core = lax.div(c, 2), lax.rem(c, 2)
    chips = cols // 2
    q0, k0 = lax.div(r, 2), lax.rem(r, 2)
    pa = lax.rem(r, 2)
    pb = 1 - pa
    mate = r + 1 - 2 * pa
    on_line = core == k0
    diag = (q == q0) & on_line
    has_up = on_line & (q >= q0) & (q + 1 < chips)
    has_dn = on_line & (q <= q0) & (q > 0)
    chip_hops = jnp.where(q >= q0, q - q0, q0 - q)

    def load_a(s, i):
        return pltpu.make_async_copy(
            inv_hbm.at[0, s, pl.ds(i * AB, AB), pl.ds(i * AB, order - i * AB)],
            a_buf.at[s, pl.ds(i * AB, AB), pl.ds(i * AB, order - i * AB)],
            a_sem.at[s, i])

    def load_m(s):
        return pltpu.make_async_copy(cpl_hbm.at[0, s], m_buf.at[s], m_sem.at[s])

    load_slab = pltpu.make_async_copy(slab_hbm, slab, s_sem)
    for s in range(subs):
        load_m(s).start()
        for i in range(ablocks):
            load_a(s, i).start()
    load_slab.start()

    barrier = pltpu.get_barrier_semaphore()
    for t in range(rows):
        @pl.when(t != r)
        def _():
            pl.semaphore_signal(barrier, inc=1, device_id=(t, c), device_id_type=MESH)
    pl.semaphore_signal(barrier, inc=1, device_id=(r, c + 1 - 2 * core), device_id_type=MESH)

    @pl.when(q + 1 < chips)
    def _():
        pl.semaphore_signal(barrier, inc=1, device_id=(r, c + 2), device_id_type=MESH)

    @pl.when(q > 0)
    def _():
        pl.semaphore_signal(barrier, inc=1, device_id=(r, c - 2), device_id_type=MESH)

    for k in range(pivots.shape[0]):
        piv[pl.ds(k * 128, 128), :] = jnp.transpose(
            jnp.broadcast_to(pivots[pl.ds(k, 1), :], (128, 128)))
    for t in range(rows):
        for k in range(nb + 1):
            placed[t, k * (nb + 1) + nb] = jnp.zeros((unit, unit), BF16)
            placed[t, nb * (nb + 1) + k] = jnp.zeros((unit, unit), BF16)

    neighbours = rows + jnp.where(q + 1 < chips, 1, 0) + jnp.where(q > 0, 1, 0)
    pl.semaphore_wait(barrier, neighbours)

    def pick(src, dst):
        found, which = jnp.int32(0), jnp.int32(0)
        for s in range(subs):
            hit = owners[src, 0, s] == dst
            found, which = jnp.where(hit, 1, found), jnp.where(hit, s, which)
        return found, which

    def tile_copy(t, src_row):
        return pltpu.make_async_remote_copy(
            src_ref=send.at[t], dst_ref=recv.at[src_row],
            send_sem=t_send.at[t], recv_sem=t_recv.at[src_row],
            device_id=(t, c), device_id_type=MESH)

    for s in range(subs):
        load_m(s).wait()
        for i in range(ablocks):
            load_a(s, i).wait()

    for t in range(rows):
        _, which = pick(r, t)
        live = lax.broadcasted_iota(jnp.int32, (order, width), 0) < orders[0, which]
        mm[...] = jnp.where(live, m_buf[which], jnp.zeros((order, width), BF16))
        for i in range(ablocks):
            lo = i * AB
            half = a_buf[which, lo:lo + AB, lo:lo + AB] * jnp.asarray(0.5, BF16)
            part = jnp.dot(half, mm[lo:lo + AB], preferred_element_type=F32)
            if i + 1 < ablocks:
                part = part + jnp.dot(a_buf[which, lo:lo + AB, lo + AB:], mm[lo + AB:],
                                      preferred_element_type=F32)
            sol[lo:lo + AB] = part.astype(BF16)
        half_tile = contract0(mm[...], sol[...])
        whole_tile = (half_tile + jnp.transpose(half_tile)).astype(BF16)
        value = jnp.stack([whole_tile[a * unit:(a + 1) * unit, b * unit:(b + 1) * unit]
                           for a, b in pairs])

        @pl.when(t != r)
        def _():
            send[t] = value
            tile_copy(t, r).start()

        @pl.when(t == r)
        def _():
            recv[t] = value

    def part(ref, p, j):
        return ref.at[p, pl.ds(pl.multiple_of(j * chunk, chunk), chunk)]

    def panel_copy(j, target, sems):
        return pltpu.make_async_remote_copy(
            src_ref=part(panel, pa, j), dst_ref=part(panel, pa, j),
            send_sem=sems.at[j], recv_sem=g_recv.at[pa, j],
            device_id=(target, c), device_id_type=MESH)

    def panel_got(p, j):
        pltpu.make_async_remote_copy(
            src_ref=part(panel, p, j), dst_ref=part(panel, p, j),
            send_sem=ax_send.at[j], recv_sem=g_recv.at[p, j],
            device_id=(mate, c), device_id_type=MESH).wait_recv()

    def send_panel(j):
        @pl.when(r + 2 < rows)
        def _():
            panel_copy(j, r + 2, ay_send).start()
        panel_copy(j, mate, ax_send).start()

    def left_copy(src, p, j, target, sems):
        return pltpu.make_async_remote_copy(
            src_ref=part(src, p, j), dst_ref=part(left, p, j),
            send_sem=sems.at[p, j], recv_sem=l_recv.at[p, j],
            device_id=(r, target), device_id_type=MESH)

    def forward(src, p, j):
        @pl.when(has_up)
        def _():
            left_copy(src, p, j, c + 2, up_send).start()

        @pl.when(has_dn)
        def _():
            left_copy(src, p, j, c - 2, dn_send).start()
        left_copy(src, p, j, c + 1 - 2 * core, core_send).start()

    load_slab.wait()
    places = []
    side = nb + 1
    for t in range(rows):
        found, which = pick(t, r)
        at_row, at_col = offsets[t, 0, which], offsets[t, 1, which]
        spots = []
        for start in (at_row, at_col):
            inside = [(found > 0) & (k - start >= 0) & (k - start < nb) for k in range(grid)]
            spots.append([jnp.where(ok, k - start, nb) for k, ok in enumerate(inside)])
        places.append(([side * a for a in spots[0]], spots[1]))

        @pl.when(t != r)
        def _():
            tile_copy(t, t).wait_recv()
    for t in range(rows):
        for k, (a, b) in enumerate(pairs):
            value = recv[t, k]
            placed[t, a * side + b] = value
            if a != b:
                placed[t, b * side + a] = jnp.transpose(value.astype(F32)).astype(BF16)
    for i in range(grid):
        for j in range(grid):
            total = slab[i * unit:(i + 1) * unit, j * unit:(j + 1) * unit]
            for t in range(rows):
                total = total - placed[t, places[t][0][i] + places[t][1][j]].astype(F32)
            out[i * unit:(i + 1) * unit, j * unit:(j + 1) * unit] = total

        @pl.when(r < 2)
        def _():
            span = slice(i * unit, (i + 1) * unit)
            panel[pa, span] = out[span, :].astype(BF16)
            for j in range(i * unit // chunk, (i + 1) * unit // chunk):
                send_panel(j)

    lanes = tile // 128
    late = 4
    off_line = jnp.where(on_line, 0, 2)
    first_left = jnp.where(diag | (r < 2), 0, 4 * chip_hops + off_line)

    def step(n, carry):
        @pl.when((n < CHUNKS) & (r >= 2))
        def _():
            panel_got(pa, n)
            send_panel(n)

        def own(p, j):
            @pl.when(diag)
            def _():
                forward(panel, p, j)
                at = pl.ds(pl.multiple_of(j * chunk, chunk), chunk)
                left[p, at] = panel[p, at]

        def other(p, j):
            @pl.when((j >= 0) & (j < CHUNKS) & jnp.logical_not(diag))
            def _():
                left_copy(left, p, j, c + 1 - 2 * core, core_send).wait_recv()

                @pl.when(on_line)
                def _():
                    forward(left, p, j)

        @pl.when(n < CHUNKS)
        def _():
            own(pa, n)
        m = n - late

        @pl.when((m >= 0) & (m < CHUNKS) & diag)
        def _():
            panel_got(pb, m)
            own(pb, m)
        other(pa, n - first_left)
        j = m - first_left
        other(pb, j)

        @pl.when((j >= 0) & jnp.logical_not(diag))
        def _():
            panel_got(pb, j)

        @pl.when((j >= 0) & (lax.rem(j, MERGE) == MERGE - 1))
        def _():
            first = pl.multiple_of((j - (MERGE - 1)) * chunk, MERGE * chunk)
            at = pl.ds(first, MERGE * chunk)
            factors, rights = [], []
            for p in range(2):
                pivot = piv[pl.ds(pl.multiple_of(p * tile + first, chunk), MERGE * chunk), :]
                raw = left[p, at].astype(F32)
                factors.append((raw / jnp.concatenate([pivot] * lanes, axis=1)).astype(BF16))
                rights.append(panel[p, at])
            factor = jnp.concatenate(factors, axis=0)
            out[...] = out[...] - contract0(factor, jnp.concatenate(rights, axis=0))
        return carry

    lax.fori_loop(0, CHUNKS + first_left + late, step, 0)

    for t in range(rows):
        @pl.when(t != r)
        def _():
            tile_copy(t, r).wait_send()

    def drain(j, carry):
        @pl.when(r + 2 < rows)
        def _():
            panel_copy(j, r + 2, ay_send).wait_send()
        panel_copy(j, mate, ax_send).wait_send()

        @pl.when(on_line)
        def _():
            for p in range(2):
                @pl.when(has_up)
                def _():
                    left_copy(left, p, j, c + 2, up_send).wait_send()

                @pl.when(has_dn)
                def _():
                    left_copy(left, p, j, c - 2, dn_send).wait_send()
                left_copy(left, p, j, c + 1 - 2 * core, core_send).wait_send()
        return carry

    lax.fori_loop(0, CHUNKS, drain, 0)


def body(rows, cols, inverses, coupling, orders, owners, offsets, dense_slab, pivots):
    subs, order = inverses.shape[1], inverses.shape[2]
    width, tile = coupling.shape[3], dense_slab.shape[0]
    unit = (tile - width) // 2
    nb = width // unit
    upper = nb * (nb + 1) // 2
    panel_width = pivots.shape[0]
    assert panel_width == 2 * tile and rows % 2 == 0 and cols % 2 == 0
    dma = pltpu.SemaphoreType.DMA
    hbm = pl.BlockSpec(memory_space=pl.ANY)
    smem = pl.BlockSpec(memory_space=pltpu.SMEM)
    vmem = pl.BlockSpec(memory_space=pltpu.VMEM)
    return pl.pallas_call(
        functools.partial(kernel, (rows, cols, subs, order, width, tile)),
        out_shape=pltpu.VMEM((tile, tile), F32),
        in_specs=[hbm, hbm, smem, smem, smem, hbm, vmem],
        out_specs=vmem,
        scratch_shapes=[
            pltpu.VMEM((subs, order, order), BF16),
            pltpu.VMEM((subs, order, width), BF16),
            pltpu.VMEM((tile, tile), F32),
            pltpu.VMEM((order, width), BF16),
            pltpu.VMEM((order, width), BF16),
            pltpu.VMEM((rows, upper, unit, unit), BF16),
            pltpu.VMEM((rows, upper, unit, unit), BF16),
            pltpu.VMEM((rows, (nb + 1) * (nb + 1), unit, unit), BF16),
            pltpu.VMEM((2, tile, tile), BF16),
            pltpu.VMEM((2, tile, tile), BF16),
            pltpu.VMEM((panel_width, 128), F32),
            dma((subs, order // AB)), dma((subs,)), dma(()),
            dma((rows,)), dma((rows,)),
            dma((CHUNKS,)), dma((CHUNKS,)), dma((2, CHUNKS)),
            dma((2, CHUNKS)), dma((2, CHUNKS)), dma((2, CHUNKS)), dma((2, CHUNKS)),
        ],
        compiler_params=pltpu.CompilerParams(collective_id=0, has_side_effects=True),
    )(inverses, coupling, orders, jnp.transpose(owners, (0, 2, 1)),
      jnp.transpose(offsets, (0, 2, 1)), dense_slab, pivots.reshape(-1, 128))


def solution(mesh):
    placed = (
        P("row", "col", None, None),
        P("row", "col", None, None),
        P("row", "col"),
        P(None, "col", None),
        P(None, "col", None),
        P("row", "col"),
        P(),
    )
    return jax.shard_map(
        functools.partial(body, mesh.shape["row"], mesh.shape["col"]),
        mesh=mesh, in_specs=placed, out_specs=P("row", "col"), check_vma=False)
```
